32 devices in a mesh: pipe: 8 (over y, x, core), sp: 4 (over z).
Axes of the slice: x: 2, y: 2, z: 4, core: 2. Of those that a mesh axis runs over, the one named last changes fastest.
Arguments:
- queries: bfloat16 [8, 512, 8192], P('pipe', 'sp'), may hold values from -48 to 48, as said below
- keys_values: bfloat16 [8, 512, 2048], P('pipe', 'sp'), may hold values from -8 to 8
- first_tile: int32 [8, 4], P('pipe'), may hold values from 0 to 3, as said below
Outputs:
- next_input: bfloat16 [8, 512, 8192], P('pipe', 'sp')
The draws below stay inside these ranges and needn't reach their ends.
Inputs may be any that keep to these rules, and one draw needn't show every extreme that they name: queries[s, i, :] and keys_values[s, j, :] are of order one in most rows; a few rows are much larger. first_tile[s, t] is the first tile of the document that holds tile t of section s: first_tile[s, 0] = 0, first_tile[s, t] is t or first_tile[s, t - 1], and the last tile 4 - 1 begins a document.
All inputs are finite; a program needn't handle non-finite values.
Results may differ from the reference program's by a relative error of at most 0.0046.
Values may be sent and summed in bfloat16 or wider, within the bound.
A program may use at most 64 MiB of HBM per device.

```python
import math
import jax
import jax.numpy as jnp
from jax import lax

H = 64
KVH = 8
DH = 128
TILE = 128
SEQ = 512
TILES = 4
SECTIONS = 8


def paired_draw(key):
    subkeys = jax.random.split(jax.random.fold_in(key, 17), 2)
    kv_normal = jnp.clip(jax.random.normal(subkeys[0], (SECTIONS, SEQ, KVH, 2, DH), jnp.float32), -4.0, 4.0)
    query_normal = jnp.clip(jax.random.normal(subkeys[1], (SECTIONS, SEQ, H, DH), jnp.float32), -4.0, 4.0)
    keys_only = kv_normal[:, :, :, 0, :]
    values_only = kv_normal[:, :, :, 1, :]
    kv_full = jnp.stack([keys_only, values_only], axis=3).reshape(SECTIONS, SEQ, KVH * 2 * DH)
    return (query_normal.reshape(SECTIONS, SEQ, H * DH), kv_full)


def draw_queries(key, part):
    return paired_draw(key)[0].astype(jnp.bfloat16)


def draw_keys_values(key, part):
    return paired_draw(key)[1].astype(jnp.bfloat16)


def draw_first_tile(key, part):
    flags = jax.random.randint(jax.random.fold_in(key, 29), (SECTIONS, TILES), 0, 4) == 0
    tile_ids = jnp.arange(TILES, dtype=jnp.int32)[None, :]
    flags = flags | (tile_ids == 0) | (tile_ids == TILES - 1)
    starts = jnp.where(flags, tile_ids, 0).astype(jnp.int32)
    return lax.cummax(starts, axis=1).astype(jnp.int32)


def setup_inputs(seed: int = 0) -> dict:
    seeds = jax.random.split(jax.random.key(seed), 4)
    queries = draw_queries(jax.random.fold_in(seeds[3], 71), 0)
    keys_values = draw_keys_values(jax.random.fold_in(seeds[3], 71), 0)
    first_tile = draw_first_tile(jax.random.fold_in(seeds[3], 71), 0)
    return dict(queries=queries, keys_values=keys_values, first_tile=first_tile)


def attend_heads(query_part, key_value_part, row_start):
    seq_len = query_part.shape[0]
    dim_head = query_part.shape[-1]
    block_rows = seq_len // 8
    scale_factor = 1.0 / math.sqrt(dim_head)
    key_part = key_value_part[..., :dim_head].astype(jnp.float32)
    value_part = key_value_part[..., dim_head:].astype(jnp.float32)
    pieces = []
    for block_index in range(8):
        begin_row = block_index * block_rows
        end_row = begin_row + block_rows
        scores = jnp.einsum('ikgd,jkd->kgij', query_part[begin_row:end_row].astype(jnp.float32), key_part[:end_row]) * scale_factor
        row_ids = jnp.arange(begin_row, end_row, dtype=jnp.int32)[:, None]
        col_ids = jnp.arange(end_row, dtype=jnp.int32)[None, :]
        visible = (col_ids <= row_ids) & (col_ids >= row_start[begin_row:end_row][:, None])
        scores = jnp.where(visible, scores, -jnp.inf)
        largest = lax.optimization_barrier(jnp.max(scores, axis=-1, keepdims=True))
        exponent_terms = jnp.exp(scores - largest)
        weights = lax.optimization_barrier((exponent_terms / lax.optimization_barrier(jnp.sum(exponent_terms, axis=-1, keepdims=True))).astype(jnp.bfloat16))
        attended = jnp.einsum('kgij,jkd->ikgd', weights.astype(jnp.float32), value_part[:end_row])
        pieces.append(attended.astype(jnp.bfloat16))
    return jnp.concatenate(pieces, axis=0)

def reference(queries, keys_values, first_tile):
    group_size = H // KVH

    def one_section(section_args):
        section_queries, section_kv, section_first = section_args
        seq_len = section_queries.shape[0]
        row_start = jnp.repeat(section_first * TILE, TILE).astype(jnp.int32)
        query_part = section_queries.reshape(seq_len, KVH, group_size, DH)
        kv_part = section_kv.reshape(seq_len, KVH, 2 * DH)
        return attend_heads(query_part, kv_part, row_start).reshape(seq_len, H * DH)
    attended = lax.map(one_section, (queries, keys_values, first_tile))
    return jnp.roll(attended, 1, axis=0)
```

```python
import functools
import math

import jax
import jax.numpy as jnp
from jax import lax
from jax.experimental import pallas as pl
from jax.experimental.pallas import tpu as pltpu
from jax.sharding import PartitionSpec as P

H = 64
KVH = 8
DH = 128
REP = H // KVH
QW = REP * DH
KW = 2 * DH
UNROLL_TILES = 3
MESH = pl.DeviceIdType.MESH


def scores_of(query, key):
    return lax.dot_general(
        query, key, (((1,), (1,)), ((), ())), preferred_element_type=jnp.float32
    )


def kernel(n_pipe, n_sp, first_ref, q_hbm, kv_hbm, out_hbm, q_buf, own, kv_buf, staged,
           q_sem, own_sem, kv_send, kv_recv, out_send, out_recv):
    sp = lax.axis_index("sp")
    pipe = lax.axis_index("pipe")
    after = lax.rem(pipe + 1, n_pipe)
    before = lax.rem(pipe + n_pipe - 1, n_pipe)
    rows = q_buf.shape[0]
    last = n_sp - 1
    n_before = jnp.where(sp == last, 0, sp)

    def q_cols(g):
        return pl.ds(pl.multiple_of(g * QW, QW), QW)

    def kv_cols(g):
        return pl.ds(pl.multiple_of(g * KW, KW), KW)

    def q_copy(g):
        return pltpu.make_async_copy(q_hbm.at[0, :, q_cols(g)], q_buf.at[:, q_cols(g)], q_sem.at[g])

    def kv_copy(g, source, target):
        return pltpu.make_async_remote_copy(
            src_ref=kv_hbm.at[0, :, kv_cols(g)],
            dst_ref=kv_buf.at[source, :, kv_cols(g)],
            send_sem=kv_send.at[target, g],
            recv_sem=kv_recv.at[source, g],
            device_id={"sp": target},
            device_id_type=MESH,
        )

    def out_copy(g):
        return pltpu.make_async_remote_copy(
            src_ref=staged.at[:, q_cols(g)],
            dst_ref=out_hbm.at[0, :, q_cols(g)],
            send_sem=out_send.at[g],
            recv_sem=out_recv.at[g],
            device_id={"pipe": after},
            device_id_type=MESH,
        )

    barrier = pltpu.get_barrier_semaphore()
    for neighbour in (after, before):
        pl.semaphore_signal(barrier, inc=1, device_id={"pipe": neighbour}, device_id_type=MESH)
    for step in range(1, n_sp):
        pl.semaphore_signal(
            barrier, inc=1, device_id={"sp": lax.rem(sp + step, n_sp)}, device_id_type=MESH
        )
    own_copy = pltpu.make_async_copy(kv_hbm.at[0], own, own_sem)
    own_copy.start()
    for g in range(KVH):
        q_copy(g).start()
    pl.semaphore_wait(barrier, 2 + n_sp - 1)

    @pl.loop(0, KVH)
    def _(g):
        for target in range(last - 1, 0, -1):
            @pl.when(target > sp)
            def _():
                kv_copy(g, sp, target).start()

    own_copy.wait()
    first = first_ref[0, sp]
    factor = math.log2(math.e) / math.sqrt(DH)
    row_ids = lax.broadcasted_iota(jnp.int32, (rows, rows), 0)
    col_ids = lax.broadcasted_iota(jnp.int32, (rows, rows), 1)

    def bias_of(tile):
        return jnp.where(tile >= first, 0.0, -jnp.inf).astype(jnp.float32)

    def whole_softmax(g, count):
        k_cols = pl.ds(pl.multiple_of(g * KW, DH), DH)
        v_cols = pl.ds(pl.multiple_of(g * KW + DH, DH), DH)
        for head in range(REP):
            cols = pl.ds(pl.multiple_of(g * QW + head * DH, DH), DH)
            query = q_buf[:, cols]
            parts = [
                scores_of(query, kv_buf[tile, :, k_cols]) + bias_of(tile) for tile in range(count)
            ]
            parts.append(jnp.where(col_ids <= row_ids, scores_of(query, own[:, k_cols]), -jnp.inf))
            largest = jnp.max(functools.reduce(jnp.maximum, parts), axis=-1, keepdims=True)
            terms = [jnp.exp2((part - largest) * factor) for part in parts]
            total = jnp.sum(functools.reduce(jnp.add, terms), axis=-1, keepdims=True)
            share = 1.0 / total
            values = [kv_buf[tile, :, v_cols] for tile in range(count)] + [own[:, v_cols]]
            result = sum(
                jnp.dot((term * share).astype(jnp.bfloat16), value,
                        preferred_element_type=jnp.float32)
                for term, value in zip(terms, values)
            )
            staged[:, cols] = result.astype(jnp.bfloat16)

    def running_softmax(g):
        k_cols = pl.ds(pl.multiple_of(g * KW, DH), DH)
        v_cols = pl.ds(pl.multiple_of(g * KW + DH, DH), DH)

        @pl.loop(0, REP)
        def _(head):
            cols = pl.ds(pl.multiple_of(g * QW + head * DH, DH), DH)
            query = q_buf[:, cols]
            score = jnp.where(col_ids <= row_ids, scores_of(query, own[:, k_cols]), -jnp.inf)
            largest = jnp.max(score, axis=-1, keepdims=True)
            term = jnp.exp2((score - largest) * factor)
            total = jnp.sum(term, axis=-1, keepdims=True)
            result = jnp.dot(term.astype(jnp.bfloat16), own[:, v_cols],
                             preferred_element_type=jnp.float32)

            def step(tile, carry):
                largest, total, result = carry
                score = scores_of(query, kv_buf[tile, :, k_cols]) + bias_of(tile)
                larger = jnp.maximum(largest, jnp.max(score, axis=-1, keepdims=True))
                shrink = jnp.exp2((largest - larger) * factor)
                term = jnp.exp2((score - larger) * factor)
                total = total * shrink + jnp.sum(term, axis=-1, keepdims=True)
                result = result * shrink + jnp.dot(
                    term.astype(jnp.bfloat16), kv_buf[tile, :, v_cols],
                    preferred_element_type=jnp.float32)
                return larger, total, result

            _, total, result = lax.fori_loop(0, n_before, step, (largest, total, result))
            staged[:, cols] = (result / total).astype(jnp.bfloat16)

    @pl.loop(0, KVH)
    def _(g):
        q_copy(g).wait()
        for tile in range(last - 1):
            @pl.when(tile < n_before)
            def _():
                kv_copy(g, tile, sp).wait_recv()
        if last <= UNROLL_TILES:
            for count in range(max(last, 1)):
                @pl.when(n_before == count)
                def _():
                    whole_softmax(g, count)
        else:
            running_softmax(g)
        out_copy(g).start()

    @pl.loop(0, KVH)
    def _(g):
        for target in range(last - 1, 0, -1):
            @pl.when(target > sp)
            def _():
                kv_copy(g, sp, target).wait_send()
        out_copy(g).wait()


def per_device(n_pipe, n_sp, queries, keys_values, first_tile):
    rows = queries.shape[1]
    tiles = n_sp
    return pl.pallas_call(
        functools.partial(kernel, n_pipe, n_sp),
        out_shape=jax.ShapeDtypeStruct(queries.shape, jnp.bfloat16),
        in_specs=[
            pl.BlockSpec(memory_space=pltpu.SMEM),
            pl.BlockSpec(memory_space=pl.ANY),
            pl.BlockSpec(memory_space=pl.ANY),
        ],
        out_specs=pl.BlockSpec(memory_space=pl.ANY),
        scratch_shapes=[
            pltpu.VMEM((rows, H * DH), jnp.bfloat16),
            pltpu.VMEM((rows, KVH * KW), jnp.bfloat16),
            pltpu.VMEM((max(tiles - 2, 1), rows, KVH * KW), jnp.bfloat16),
            pltpu.VMEM((rows, H * DH), jnp.bfloat16),
            pltpu.SemaphoreType.DMA((KVH,)),
            pltpu.SemaphoreType.DMA,
            pltpu.SemaphoreType.DMA((tiles, KVH)),
            pltpu.SemaphoreType.DMA((tiles, KVH)),
            pltpu.SemaphoreType.DMA((KVH,)),
            pltpu.SemaphoreType.DMA((KVH,)),
        ],
        compiler_params=pltpu.CompilerParams(
            collective_id=0, has_side_effects=True, vmem_limit_bytes=40 * 1024 * 1024
        ),
    )(first_tile, queries, keys_values)


def solution(mesh):
    sizes = dict(mesh.shape)
    in_specs = (P("pipe", "sp", None), P("pipe", "sp", None), P("pipe", None))
    out_specs = P("pipe", "sp", None)
    return jax.shard_map(
        functools.partial(per_device, sizes["pipe"], sizes["sp"]),
        mesh=mesh, in_specs=in_specs, out_specs=out_specs, check_vma=False,
    )
```

```python
import functools
import math

import jax
import jax.numpy as jnp
from jax import lax
from jax.experimental import pallas as pl
from jax.experimental.pallas import tpu as pltpu
from jax.sharding import PartitionSpec as P

H = 64
KVH = 8
DH = 128
REP = H // KVH
QW = REP * DH
KW = 2 * DH
UNROLL_TILES = 3
STACK = 8
MESH = pl.DeviceIdType.MESH


def scores_of(query, key):
    return lax.dot_general(
        query, key, (((1,), (1,)), ((), ())), preferred_element_type=jnp.float32
    )


def kernel(n_pipe, n_sp, first_hbm, q_hbm, kv_hbm, out_hbm, first_ref, q_buf, own, kv_buf, staged,
           first_sem, q_sem, own_sem, kv_send, kv_recv, out_send, out_recv):
    sp = lax.axis_index("sp")
    pipe = lax.axis_index("pipe")
    after = lax.rem(pipe + 1, n_pipe)
    before = lax.rem(pipe + n_pipe - 1, n_pipe)
    rows = q_buf.shape[0]
    last = n_sp - 1
    n_before = jnp.where(sp == last, 0, sp)

    def q_cols(g):
        return pl.ds(pl.multiple_of(g * QW, QW), QW)

    def kv_cols(g):
        return pl.ds(pl.multiple_of(g * KW, KW), KW)

    def q_copy(g):
        return pltpu.make_async_copy(q_hbm.at[0, :, q_cols(g)], q_buf.at[:, q_cols(g)], q_sem.at[g])

    def kv_copy(g, source, target):
        return pltpu.make_async_remote_copy(
            src_ref=kv_hbm.at[0, :, kv_cols(g)],
            dst_ref=kv_buf.at[source, :, kv_cols(g)],
            send_sem=kv_send.at[target, g],
            recv_sem=kv_recv.at[source, g],
            device_id={"sp": target},
            device_id_type=MESH,
        )

    def out_copy(g):
        return pltpu.make_async_remote_copy(
            src_ref=staged.at[:, q_cols(g)],
            dst_ref=out_hbm.at[0, :, q_cols(g)],
            send_sem=out_send.at[g],
            recv_sem=out_recv.at[g],
            device_id={"pipe": after},
            device_id_type=MESH,
        )

    barrier = pltpu.get_barrier_semaphore()
    for neighbour in (after, before):
        pl.semaphore_signal(barrier, inc=1, device_id={"pipe": neighbour}, device_id_type=MESH)
    for step in range(1, n_sp):
        pl.semaphore_signal(
            barrier, inc=1, device_id={"sp": lax.rem(sp + step, n_sp)}, device_id_type=MESH
        )
    own_copy = pltpu.make_async_copy(kv_hbm.at[0], own, own_sem)
    own_copy.start()
    first_copy = pltpu.make_async_copy(first_hbm, first_ref, first_sem)
    first_copy.start()
    for g in range(KVH):
        q_copy(g).start()
    pl.semaphore_wait(barrier, 2 + n_sp - 1)

    @pl.loop(0, KVH)
    def _(g):
        for target in range(last - 1, 0, -1):
            @pl.when(target > sp)
            def _():
                kv_copy(g, sp, target).start()

    own_copy.wait()
    first_copy.wait()
    first = first_ref[0, sp]
    factor = math.log2(math.e) / math.sqrt(DH)
    row_ids = lax.broadcasted_iota(jnp.int32, (rows, rows), 0)
    col_ids = lax.broadcasted_iota(jnp.int32, (rows, rows), 1)

    def bias_of(tile):
        return jnp.where(tile >= first, 0.0, -jnp.inf).astype(jnp.float32)

    def whole_softmax(g, count):
        k_cols = pl.ds(pl.multiple_of(g * KW, DH), DH)
        v_cols = pl.ds(pl.multiple_of(g * KW + DH, DH), DH)
        for begin in range(0, REP, STACK):
            cols = [
                pl.ds(pl.multiple_of(g * QW + head * DH, DH), DH)
                for head in range(begin, begin + STACK)
            ]
            query = jnp.concatenate([q_buf[:, c] for c in cols], axis=0)
            parts = [
                scores_of(query, kv_buf[tile, :, k_cols]) + bias_of(tile) for tile in range(count)
            ]
            score = scores_of(query, own[:, k_cols]).reshape(STACK, rows, rows)
            score = jnp.where((col_ids <= row_ids)[None], score, -jnp.inf)
            parts.append(score.reshape(STACK * rows, rows))
            largest = jnp.max(functools.reduce(jnp.maximum, parts), axis=-1, keepdims=True)
            terms = [jnp.exp2((part - largest) * factor) for part in parts]
            total = jnp.sum(functools.reduce(jnp.add, terms), axis=-1, keepdims=True)
            share = 1.0 / total
            values = [kv_buf[tile, :, v_cols] for tile in range(count)] + [own[:, v_cols]]
            result = sum(
                jnp.dot((term * share).astype(jnp.bfloat16), value,
                        preferred_element_type=jnp.float32)
                for term, value in zip(terms, values)
            ).astype(jnp.bfloat16)
            for index, c in enumerate(cols):
                staged[:, c] = result[index * rows:(index + 1) * rows]

    def running_softmax(g):
        k_cols = pl.ds(pl.multiple_of(g * KW, DH), DH)
        v_cols = pl.ds(pl.multiple_of(g * KW + DH, DH), DH)

        @pl.loop(0, REP)
        def _(head):
            cols = pl.ds(pl.multiple_of(g * QW + head * DH, DH), DH)
            query = q_buf[:, cols]
            score = jnp.where(col_ids <= row_ids, scores_of(query, own[:, k_cols]), -jnp.inf)
            largest = jnp.max(score, axis=-1, keepdims=True)
            term = jnp.exp2((score - largest) * factor)
            total = jnp.sum(term, axis=-1, keepdims=True)
            result = jnp.dot(term.astype(jnp.bfloat16), own[:, v_cols],
                             preferred_element_type=jnp.float32)

            def step(tile, carry):
                largest, total, result = carry
                score = scores_of(query, kv_buf[tile, :, k_cols]) + bias_of(tile)
                larger = jnp.maximum(largest, jnp.max(score, axis=-1, keepdims=True))
                shrink = jnp.exp2((largest - larger) * factor)
                term = jnp.exp2((score - larger) * factor)
                total = total * shrink + jnp.sum(term, axis=-1, keepdims=True)
                result = result * shrink + jnp.dot(
                    term.astype(jnp.bfloat16), kv_buf[tile, :, v_cols],
                    preferred_element_type=jnp.float32)
                return larger, total, result

            _, total, result = lax.fori_loop(0, n_before, step, (largest, total, result))
            staged[:, cols] = (result / total).astype(jnp.bfloat16)

    @pl.loop(0, KVH)
    def _(g):
        q_copy(g).wait()
        for tile in range(last - 1):
            @pl.when(tile < n_before)
            def _():
                kv_copy(g, tile, sp).wait_recv()
        if last <= UNROLL_TILES:
            for count in range(max(last, 1)):
                @pl.when(n_before == count)
                def _():
                    whole_softmax(g, count)
        else:
            running_softmax(g)
        out_copy(g).start()

    @pl.loop(0, KVH)
    def _(g):
        for target in range(last - 1, 0, -1):
            @pl.when(target > sp)
            def _():
                kv_copy(g, sp, target).wait_send()
        out_copy(g).wait()


def per_device(n_pipe, n_sp, queries, keys_values, first_tile):
    rows = queries.shape[1]
    tiles = n_sp
    return pl.pallas_call(
        functools.partial(kernel, n_pipe, n_sp),
        out_shape=jax.ShapeDtypeStruct(queries.shape, jnp.bfloat16),
        in_specs=[
            pl.BlockSpec(memory_space=pltpu.HBM),
            pl.BlockSpec(memory_space=pltpu.HBM),
            pl.BlockSpec(memory_space=pltpu.HBM),
        ],
        out_specs=pl.BlockSpec(memory_space=pl.ANY),
        scratch_shapes=[
            pltpu.SMEM(first_tile.shape, jnp.int32),
            pltpu.VMEM((rows, H * DH), jnp.bfloat16),
            pltpu.VMEM((rows, KVH * KW), jnp.bfloat16),
            pltpu.VMEM((max(tiles - 2, 1), rows, KVH * KW), jnp.bfloat16),
            pltpu.VMEM((rows, H * DH), jnp.bfloat16),
            pltpu.SemaphoreType.DMA,
            pltpu.SemaphoreType.DMA((KVH,)),
            pltpu.SemaphoreType.DMA,
            pltpu.SemaphoreType.DMA((tiles, KVH)),
            pltpu.SemaphoreType.DMA((tiles, KVH)),
            pltpu.SemaphoreType.DMA((KVH,)),
            pltpu.SemaphoreType.DMA((KVH,)),
        ],
        compiler_params=pltpu.CompilerParams(
            collective_id=0, has_side_effects=True, vmem_limit_bytes=40 * 1024 * 1024
        ),
    )(
        pltpu.with_memory_space_constraint(first_tile, pltpu.HBM),
        pltpu.with_memory_space_constraint(queries, pltpu.HBM),
        pltpu.with_memory_space_constraint(keys_values, pltpu.HBM),
    )


def solution(mesh):
    sizes = dict(mesh.shape)
    in_specs = (P("pipe", "sp", None), P("pipe", "sp", None), P("pipe", None))
    out_specs = P("pipe", "sp", None)
    return jax.shard_map(
        functools.partial(per_device, sizes["pipe"], sizes["sp"]),
        mesh=mesh, in_specs=in_specs, out_specs=out_specs, check_vma=False,
    )
```

```python
import functools
import math

import jax
import jax.numpy as jnp
from jax import lax
from jax.experimental import pallas as pl
from jax.experimental.pallas import tpu as pltpu
from jax.sharding import PartitionSpec as P

H = 64
KVH = 8
DH = 128
REP = H // KVH
QW = REP * DH
KW = 2 * DH
UNROLL_TILES = 3
STACK = 4
CHUNKS = REP // STACK
CW = STACK * DH
TURN_GROUP = 2
MESH = pl.DeviceIdType.MESH


def scores_of(query, key):
    return lax.dot_general(
        query, key, (((1,), (1,)), ((), ())), preferred_element_type=jnp.float32
    )


def kernel(n_pipe, n_sp, first_hbm, q_hbm, kv_hbm, out_hbm, first_ref, q_buf, own, kv_buf, staged,
           turn, first_sem, q_sem, own_sem, kv_send, kv_recv, out_send, out_recv):
    sp = lax.axis_index("sp")
    pipe = lax.axis_index("pipe")
    after = lax.rem(pipe + 1, n_pipe)
    before = lax.rem(pipe + n_pipe - 1, n_pipe)
    rows = q_buf.shape[0]
    last = n_sp - 1
    n_before = jnp.where(sp == last, 0, sp)

    def q_cols(g):
        return pl.ds(pl.multiple_of(g * QW, QW), QW)

    def kv_cols(g):
        return pl.ds(pl.multiple_of(g * KW, KW), KW)

    def q_copy(g):
        return pltpu.make_async_copy(q_hbm.at[0, :, q_cols(g)], q_buf.at[:, q_cols(g)], q_sem.at[g])

    def kv_copy(g, source, target):
        return pltpu.make_async_remote_copy(
            src_ref=kv_hbm.at[0, :, kv_cols(g)],
            dst_ref=kv_buf.at[source, :, kv_cols(g)],
            send_sem=kv_send.at[target, g],
            recv_sem=kv_recv.at[source, g],
            device_id={"sp": target},
            device_id_type=MESH,
        )

    def out_copy(c):
        cols = pl.ds(pl.multiple_of(c * CW, CW), CW)
        return pltpu.make_async_remote_copy(
            src_ref=staged.at[:, cols],
            dst_ref=out_hbm.at[0, :, cols],
            send_sem=out_send.at[c],
            recv_sem=out_recv.at[c],
            device_id={"pipe": after},
            device_id_type=MESH,
        )

    barrier = pltpu.get_barrier_semaphore()
    for neighbour in (after, before):
        pl.semaphore_signal(barrier, inc=1, device_id={"pipe": neighbour}, device_id_type=MESH)
    for step in range(1, last):
        @pl.when(sp < last)
        def _():
            pl.semaphore_signal(
                barrier, inc=1, device_id={"sp": lax.rem(sp + step, last)}, device_id_type=MESH
            )
    own_copy = pltpu.make_async_copy(kv_hbm.at[0], own, own_sem)
    own_copy.start()
    first_copy = pltpu.make_async_copy(first_hbm, first_ref, first_sem)
    first_copy.start()
    for g in range(KVH):
        q_copy(g).start()
    pl.semaphore_wait(barrier, jnp.where(sp < last, last + 1, 2))

    paired = n_pipe % 2 == 0
    odd = lax.rem(pipe, 2) == 1
    sends = sp < last - 1

    if paired:
        @pl.when(sends & jnp.logical_not(odd))
        def _():
            pl.semaphore_wait(turn, 1)

    @pl.loop(0, KVH)
    def _(g):
        for target in range(last - 1, 0, -1):
            @pl.when(target > sp)
            def _():
                kv_copy(g, sp, target).start()

    own_copy.wait()
    first_copy.wait()
    first = first_ref[0, sp]
    factor = math.log2(math.e) / math.sqrt(DH)
    row_ids = lax.broadcasted_iota(jnp.int32, (rows, rows), 0)
    col_ids = lax.broadcasted_iota(jnp.int32, (rows, rows), 1)

    def bias_of(tile):
        return jnp.where(tile >= first, 0.0, -jnp.inf).astype(jnp.float32)

    def whole_softmax(g, count):
        k_cols = pl.ds(pl.multiple_of(g * KW, DH), DH)
        v_cols = pl.ds(pl.multiple_of(g * KW + DH, DH), DH)
        for begin in range(0, REP, STACK):
            cols = [
                pl.ds(pl.multiple_of(g * QW + head * DH, DH), DH)
                for head in range(begin, begin + STACK)
            ]
            query = jnp.concatenate([q_buf[:, c] for c in cols], axis=0)
            parts = [
                scores_of(query, kv_buf[tile, :, k_cols]) + bias_of(tile) for tile in range(count)
            ]
            score = scores_of(query, own[:, k_cols]).reshape(STACK, rows, rows)
            score = jnp.where((col_ids <= row_ids)[None], score, -jnp.inf)
            parts.append(score.reshape(STACK * rows, rows))
            largest = jnp.max(functools.reduce(jnp.maximum, parts), axis=-1, keepdims=True)
            terms = [jnp.exp2((part - largest) * factor) for part in parts]
            total = jnp.sum(functools.reduce(jnp.add, terms), axis=-1, keepdims=True)
            share = 1.0 / total
            values = [kv_buf[tile, :, v_cols] for tile in range(count)] + [own[:, v_cols]]
            result = sum(
                jnp.dot((term * share).astype(jnp.bfloat16), value,
                        preferred_element_type=jnp.float32)
                for term, value in zip(terms, values)
            ).astype(jnp.bfloat16)
            for index, c in enumerate(cols):
                staged[:, c] = result[index * rows:(index + 1) * rows]
            out_copy(g * CHUNKS + begin // STACK).start()

    def running_softmax(g):
        k_cols = pl.ds(pl.multiple_of(g * KW, DH), DH)
        v_cols = pl.ds(pl.multiple_of(g * KW + DH, DH), DH)

        @pl.loop(0, REP)
        def _(head):
            cols = pl.ds(pl.multiple_of(g * QW + head * DH, DH), DH)
            query = q_buf[:, cols]
            score = jnp.where(col_ids <= row_ids, scores_of(query, own[:, k_cols]), -jnp.inf)
            largest = jnp.max(score, axis=-1, keepdims=True)
            term = jnp.exp2((score - largest) * factor)
            total = jnp.sum(term, axis=-1, keepdims=True)
            result = jnp.dot(term.astype(jnp.bfloat16), own[:, v_cols],
                             preferred_element_type=jnp.float32)

            def step(tile, carry):
                largest, total, result = carry
                score = scores_of(query, kv_buf[tile, :, k_cols]) + bias_of(tile)
                larger = jnp.maximum(largest, jnp.max(score, axis=-1, keepdims=True))
                shrink = jnp.exp2((largest - larger) * factor)
                term = jnp.exp2((score - larger) * factor)
                total = total * shrink + jnp.sum(term, axis=-1, keepdims=True)
                result = result * shrink + jnp.dot(
                    term.astype(jnp.bfloat16), kv_buf[tile, :, v_cols],
                    preferred_element_type=jnp.float32)
                return larger, total, result

            _, total, result = lax.fori_loop(0, n_before, step, (largest, total, result))
            staged[:, cols] = (result / total).astype(jnp.bfloat16)

    @pl.loop(0, KVH)
    def _(g):
        q_copy(g).wait()
        for tile in range(last - 1):
            @pl.when(tile < n_before)
            def _():
                kv_copy(g, tile, sp).wait_recv()
        if last <= UNROLL_TILES:
            for count in range(max(last, 1)):
                @pl.when(n_before == count)
                def _():
                    whole_softmax(g, count)
        else:
            running_softmax(g)
            for chunk in range(CHUNKS):
                out_copy(g * CHUNKS + chunk).start()
        for target in range(last - 1, 0, -1):
            @pl.when((target > sp) & odd)
            def _():
                kv_copy(g, sp, target).wait_send()
        if paired:
            @pl.when(sends & odd & (g == TURN_GROUP))
            def _():
                pl.semaphore_signal(
                    turn, inc=1, device_id={"pipe": before}, device_id_type=MESH
                )

    @pl.loop(0, KVH)
    def _(g):
        for target in range(last - 1, 0, -1):
            @pl.when((target > sp) & jnp.logical_not(odd))
            def _():
                kv_copy(g, sp, target).wait_send()
        for chunk in range(CHUNKS):
            out_copy(g * CHUNKS + chunk).wait()


def per_device(n_pipe, n_sp, queries, keys_values, first_tile):
    rows = queries.shape[1]
    tiles = n_sp
    return pl.pallas_call(
        functools.partial(kernel, n_pipe, n_sp),
        out_shape=jax.ShapeDtypeStruct(queries.shape, jnp.bfloat16),
        in_specs=[
            pl.BlockSpec(memory_space=pltpu.HBM),
            pl.BlockSpec(memory_space=pltpu.HBM),
            pl.BlockSpec(memory_space=pltpu.HBM),
        ],
        out_specs=pl.BlockSpec(memory_space=pl.ANY),
        scratch_shapes=[
            pltpu.SMEM(first_tile.shape, jnp.int32),
            pltpu.VMEM((rows, H * DH), jnp.bfloat16),
            pltpu.VMEM((rows, KVH * KW), jnp.bfloat16),
            pltpu.VMEM((max(tiles - 2, 1), rows, KVH * KW), jnp.bfloat16),
            pltpu.VMEM((rows, H * DH), jnp.bfloat16),
            pltpu.SemaphoreType.REGULAR,
            pltpu.SemaphoreType.DMA,
            pltpu.SemaphoreType.DMA((KVH,)),
            pltpu.SemaphoreType.DMA,
            pltpu.SemaphoreType.DMA((tiles, KVH)),
            pltpu.SemaphoreType.DMA((tiles, KVH)),
            pltpu.SemaphoreType.DMA((KVH * CHUNKS,)),
            pltpu.SemaphoreType.DMA((KVH * CHUNKS,)),
        ],
        compiler_params=pltpu.CompilerParams(
            collective_id=0, has_side_effects=True, vmem_limit_bytes=40 * 1024 * 1024
        ),
    )(
        pltpu.with_memory_space_constraint(first_tile, pltpu.HBM),
        pltpu.with_memory_space_constraint(queries, pltpu.HBM),
        pltpu.with_memory_space_constraint(keys_values, pltpu.HBM),
    )


def solution(mesh):
    sizes = dict(mesh.shape)
    in_specs = (P("pipe", "sp", None), P("pipe", "sp", None), P("pipe", None))
    out_specs = P("pipe", "sp", None)
    return jax.shard_map(
        functools.partial(per_device, sizes["pipe"], sizes["sp"]),
        mesh=mesh, in_specs=in_specs, out_specs=out_specs, check_vma=False,
    )
```
